1024 devices in a mesh: section: 32 (over y_lo, z), dp: 8 (over x), fsdp: 4 (over y_hi, core).
Axes of the slice: x: 8, y: 8 (y_hi: 2, y_lo: 4; y = y_hi * 4 + y_lo), z: 8, core: 2. Of those that a mesh axis runs over, the one named last changes fastest.
Arguments:
- x_down: bfloat16 [32, 8, 512, 6144], P('section', 'dp', 'fsdp'), may hold values from -6 to 6
- x_up: bfloat16 [32, 8, 512, 6144], P('section', 'dp', 'fsdp'), may hold values from -6 to 6
- w_tiles: bfloat16 [32, 2, 20, 2, 128, 128], P('section', None, 'fsdp'), as said below
- tile_rows: int32 [32, 2, 20], P('section'), may hold values from 0 to 47, as said below
- tile_cols: int32 [32, 2, 20], P('section'), may hold values from 0 to 191, as said below
- counts: int32 [32, 2, 4], P('section'), may hold values from 2 to 5, as said below
Outputs:
- tile_grads: bfloat16 [32, 20, 2, 128, 128], P('section', 'fsdp')
The draws below stay inside these ranges and needn't reach their ends.
Inputs may be any that keep to these rules, and one draw needn't show every extreme that they name: w_tiles[l, 1] equals w_tiles[(l + 16) mod 32, 0]. tile_rows[l, 1] equals tile_rows[(l + 16) mod 32, 0]; the 20 row blocks of one layer are distinct. tile_cols[l, 1] equals tile_cols[(l + 16) mod 32, 0]; every column block that a layer uses is used by exactly two of its slots. counts[l, 1] equals counts[(l + 16) mod 32, 0]; the counts of one layer are the numbers 5 - i * 5 // 4 for i < 4 in some order.
All inputs are finite; a program needn't handle non-finite values.
Results may differ from the reference program's by a relative error of at most 0.0065.
Values may be sent and summed in bfloat16 or wider, within the bound.
A program may use at most 64 MiB of HBM per device.

```python
import math
import jax
import jax.numpy as jnp
from jax import lax

D = 6144
FF = 24576
TILE = 128
CAP = 5
ROWS = 128
SECTIONS = 32
REPLICAS = 8
OWNERS = 4
SLOTS = 20
TOKROWS = 512
TOTAL = 8192


def tile_pattern(key):

    def one_layer(layer_key):
        key_rows, key_cols, key_counts, key_pairs = jax.random.split(layer_key, 4)
        row_ids = jax.random.permutation(key_rows, D // TILE)[:SLOTS].astype(jnp.int32)
        half_cols = jax.random.permutation(key_cols, FF // TILE)[:SLOTS // 2].astype(jnp.int32)
        doubled = jnp.concatenate([half_cols, half_cols])
        placing = jax.random.permutation(key_pairs, SLOTS).astype(jnp.int32)
        col_ids = jnp.zeros((SLOTS,), jnp.int32).at[placing].set(doubled)
        order = jax.random.permutation(key_counts, OWNERS).astype(jnp.int32)
        owner_counts = CAP - order * CAP // OWNERS
        return (row_ids, col_ids, owner_counts)
    layer_keys = jax.random.split(jax.random.fold_in(key, 11), SECTIONS)
    row_ids, col_ids, owner_counts = jax.vmap(one_layer)(layer_keys)

    def paired(values):
        return jnp.stack([values, jnp.roll(values, SECTIONS // 2, axis=0)], axis=1).astype(jnp.int32)
    return (paired(row_ids), paired(col_ids), paired(owner_counts))


def draw_tile_rows(key, part):
    return tile_pattern(key)[0]


def draw_tile_cols(key, part):
    return tile_pattern(key)[1]


def draw_counts(key, part):
    return tile_pattern(key)[2]


def draw_w_tiles(key, part):
    shape = (SECTIONS, SLOTS, 2, TILE, TILE)
    base = jax.random.normal(jax.random.fold_in(key, 5), shape, jnp.float32)
    base = base * TILE ** (-0.5)
    return jnp.stack([base, jnp.roll(base, SECTIONS // 2, axis=0)], axis=1).astype(jnp.bfloat16)


def level_of(own_key, shape, cuts, least, high):
    gain = 1.0
    for axis_at, blocks in cuts:
        heights = jax.random.uniform(jax.random.fold_in(jax.random.fold_in(own_key, 6), axis_at), (blocks,), jnp.float32, least / len(cuts), high / len(cuts))
        gain = gain * jnp.repeat(jnp.exp(heights), shape[axis_at] // blocks).reshape((-1,) + (1,) * (len(shape) - 1 - axis_at))
    return gain


def centred(stream_key, shape, scale, bound, cuts=(), held_as=jnp.bfloat16):
    result = jax.random.normal(stream_key, shape, jnp.float32) * scale
    if len(cuts) > 0:
        result = level_of(stream_key, shape, cuts, -0.22, 0.18) * result
    return jnp.clip(result, min=-bound, max=bound).astype(held_as)


def setup_inputs(seed: int = 0) -> dict:
    arg_keys = jax.random.split(jax.random.key(seed), 7)
    x_down = centred(arg_keys[0], (SECTIONS, REPLICAS, TOKROWS, D), 1.0, 6.0, ((0, 32), (1, 8), (2, 4)))
    x_up = centred(arg_keys[1], (SECTIONS, REPLICAS, TOKROWS, D), 1.0, 6.0, ((0, 32), (1, 8), (2, 4)))
    w_tiles = draw_w_tiles(jax.random.fold_in(arg_keys[6], 71), 0)
    tile_rows = draw_tile_rows(jax.random.fold_in(arg_keys[6], 71), 0)
    tile_cols = draw_tile_cols(jax.random.fold_in(arg_keys[6], 71), 0)
    counts = draw_counts(jax.random.fold_in(arg_keys[6], 71), 0)
    return {"x_down": x_down, "x_up": x_up, "w_tiles": w_tiles, "tile_rows": tile_rows, "tile_cols": tile_cols, "counts": counts}


tanh_scale = math.sqrt(2.0 / math.pi)
cubic_coef = 0.044715

def gelu_pair(hidden):
    inner = tanh_scale * (hidden + cubic_coef * hidden * hidden * hidden)
    tangent = jnp.tanh(inner)
    value = 0.5 * hidden * (1.0 + tangent)
    slope = 0.5 * (1.0 + tangent) + 0.5 * hidden * (1.0 - tangent * tangent) * tanh_scale * (1.0 + 3.0 * cubic_coef * hidden * hidden)
    return (value, slope)

def slot_masks(col_ids, counts_in):
    slots = col_ids.shape[0]
    owners = counts_in.shape[0]
    per_owner = slots // owners
    slot_ids = jnp.arange(slots, dtype=jnp.int32)
    owner_ids = slot_ids // per_owner
    per_slot = lax.optimization_barrier(jnp.sum(jnp.where(owner_ids[:, None] == jnp.arange(owners, dtype=jnp.int32)[None, :], counts_in[None, :], 0), axis=1))
    living = slot_ids % per_owner < per_slot
    shared = (col_ids[:, None] == col_ids[None, :]) & living[:, None] & living[None, :]
    return shared.astype(jnp.float32)

def device_term(inputs, weights, row_ids, shared, loss_scale):
    high = lax.Precision.HIGHEST
    blocks = inputs.reshape(inputs.shape[0], -1, TILE)[:, row_ids]
    wide = blocks.astype(jnp.float32)
    first_w = weights[:, 0].astype(jnp.float32)
    second_w = weights[:, 1].astype(jnp.float32)
    contrib = jnp.einsum('nsu,suv->nsv', wide, first_w, precision=high)
    hidden = jnp.einsum('st,ntv->nsv', shared, contrib, precision=high)
    value, slope = gelu_pair(hidden)
    active = lax.optimization_barrier(value.astype(jnp.bfloat16)).astype(jnp.float32)
    delta = jnp.einsum('nsu,suv->nsv', active, second_w, precision=high)
    cotangent = lax.optimization_barrier((loss_scale * (wide + delta)).astype(jnp.bfloat16)).astype(jnp.float32)
    spread = jnp.einsum('nsv,suv->nsu', cotangent, second_w, precision=high)
    grad_act = jnp.einsum('st,ntu->nsu', shared, spread, precision=high)
    grad_pre = lax.optimization_barrier((grad_act * slope).astype(jnp.bfloat16)).astype(jnp.float32)
    grad_first = jnp.einsum('nsu,nsv->suv', wide, grad_pre, precision=high)
    grad_second = jnp.einsum('nsu,nsv->suv', active, cotangent, precision=high)
    return jnp.stack([grad_first, grad_second], axis=1).astype(jnp.bfloat16)

def reference(x_down, x_up, w_tiles, tile_rows, tile_cols, counts):
    loss_scale = TOTAL ** (-0.5)

    def one_layer(layer):
        partner = (layer + SECTIONS // 2) % SECTIONS
        weights = w_tiles[layer, 0]
        row_ids = tile_rows[layer, 0]
        shared = slot_masks(tile_cols[layer, 0], counts[layer, 0])
        batches = jnp.concatenate([x_down[layer].reshape(-1, ROWS, D), x_up[partner].reshape(-1, ROWS, D)], axis=0)

        def accumulate(summed, inputs):
            piece = lax.optimization_barrier(device_term(inputs, weights, row_ids, shared, loss_scale))
            return (summed + piece.astype(jnp.float32), None)
        summed, _ = lax.scan(accumulate, jnp.zeros((SLOTS, 2, TILE, TILE), jnp.float32), batches)
        return summed.astype(jnp.bfloat16)
    return lax.map(one_layer, jnp.arange(SECTIONS, dtype=jnp.int32))
```

```python
import functools
import math

import jax
import jax.numpy as jnp
from jax import lax
from jax.experimental import pallas as pl
from jax.experimental.pallas import tpu as pltpu
from jax.sharding import PartitionSpec as P

TILE = 128
MESH = pl.DeviceIdType.MESH
WAVES = 2

tanh_scale = math.sqrt(2.0 / math.pi)
cubic_coef = 0.044715


def gelu_pair(hidden):
    inner = tanh_scale * (hidden + cubic_coef * hidden * hidden * hidden)
    tangent = jnp.tanh(inner)
    value = 0.5 * hidden * (1.0 + tangent)
    slope = 0.5 * (1.0 + tangent) + 0.5 * hidden * (1.0 - tangent * tangent) * tanh_scale * (
        1.0 + 3.0 * cubic_coef * hidden * hidden
    )
    return value, slope


def dot(a, b, ca, cb):
    return lax.dot_general(a, b, (((ca,), (cb,)), ((), ())), preferred_element_type=jnp.float32)


def slot_pairs(cols, counts):
    slots = cols.shape[1]
    per_owner = slots // counts.shape[1]
    ids = jnp.arange(slots, dtype=jnp.int32)
    live = (jnp.arange(per_owner, dtype=jnp.int32) < counts[:, :, None]).astype(jnp.int32).reshape(cols.shape)
    same = (cols[:, :, None] == cols[:, None, :]) & (ids[:, None] != ids[None, :])
    pair = jnp.sum(jnp.where(same, ids, 0), axis=2)
    other_live = jnp.sum(jnp.where(same, live[:, None, :], 0), axis=2)
    return pair, live, other_live


def pick(rows_s, x_down, x_up, out, sems):
    copies = []
    for layer, x in enumerate((x_down, x_up)):
        for s in range(out.shape[1]):
            at = pl.ds(pl.multiple_of(rows_s[layer, s] * TILE, TILE), TILE)
            copies.append(pltpu.make_async_copy(x.at[:, at], out.at[layer, s], sems.at[layer, s]))
            copies[-1].start()
    for copy in copies:
        copy.wait()


class Links:
    def __init__(self, send_sems, recv_sems):
        self.send_sems, self.recv_sems = send_sems, recv_sems
        self.started = []

    def start(self, src, dst, device):
        i = len(self.started)
        copy = pltpu.make_async_remote_copy(
            src_ref=src, dst_ref=dst, send_sem=self.send_sems.at[i], recv_sem=self.recv_sems.at[i],
            device_id=device, device_id_type=MESH,
        )
        copy.start()
        self.started.append((copy, device))
        return i

    def arrived(self, i, landing):
        device = self.started[i][1]
        pltpu.make_async_remote_copy(
            src_ref=landing, dst_ref=landing, send_sem=self.send_sems.at[i],
            recv_sem=self.recv_sems.at[i], device_id=device, device_id_type=MESH,
        ).wait_recv()

    def drain(self):
        for copy, _ in self.started:
            copy.wait_send()


def copies_of(nx):
    half = nx // 2
    return 2 * (1 + 1 + 1 + 2 + 2 + 2 + 2) + 4 + 2 * WAVES * 2 * (2 * (half - 1) + 1) + 3 * WAVES + WAVES * (nx - 1)


def kernel(nx, ns, loss_scale, pair_s, live_s, both_s, x, w, out,
           xv, wv, ct, sp, sl, gmine, gsend, grecv, gsum, slots_p, slots_m, ysend, yrecv, fin, outv,
           lsem, send_sems, recv_sems):
    f32, bf16 = jnp.float32, jnp.bfloat16
    half = nx // 2
    per_owner = w.shape[1] // (2 * TILE)
    big = w.shape[1]
    chunk_rows = big // nx
    sub = chunk_rows // WAVES
    quarter = big // 4

    me = lax.axis_index("dp")
    sec = lax.axis_index("section")
    own = lax.axis_index("fsdp")
    hi, core = own // 2, own % 2
    right = {"dp": lax.rem(me + 1, nx)}
    left = {"dp": lax.rem(me + nx - 1, nx)}
    mirror = lax.rem(sec + ns // 2, ns)
    across = lax.rem(own + 2, 4)
    sib = {"fsdp": own + 1 - 2 * core}
    y_same = {"section": mirror}
    y_cross = {"section": mirror, "fsdp": across}
    y_far = {"fsdp": across}
    peers = (right, left, sib, y_cross, y_same, y_far)

    loads = [
        pltpu.make_async_copy(w, wv.at[:, 0, 0], lsem.at[0]),
        pltpu.make_async_copy(x, xv, lsem.at[1]),
    ]
    for load in loads:
        load.start()

    barrier = pltpu.get_barrier_semaphore()
    for peer in peers:
        pl.semaphore_signal(barrier, inc=1, device_id=peer, device_id_type=MESH)
    pl.semaphore_wait(barrier, len(peers))

    links = Links(send_sems, recv_sems)

    def quart(x):
        return pl.ds(pl.multiple_of(lax.rem(x, 4) * quarter, quarter), quarter)

    def halfq(x, second):
        return pl.ds(pl.multiple_of(lax.rem(x, 4) * quarter + second * (quarter // 2), quarter // 2), quarter // 2)

    q_me, q_left, q_right = quart(me), quart(me + 3), quart(me + 1)
    q_far0, q_far1 = halfq(me + 2, 0), halfq(me + 2, 1)

    c_y, c_sib = [], []
    for layer in range(2):
        c_y.append(links.start(w.at[1 - layer, q_me], wv.at[layer, 1, 0, q_me], y_cross))
    for layer in range(2):
        c_sib.append([links.start(w.at[layer], wv.at[layer, 0, 1], sib)])

    def slot_of(k, cr, j):
        return (lax.rem(hi + k, 2) * 2 + lax.rem(core + cr, 2)) * per_owner + j

    c_r, c_l, c_fr, c_fl = [], [], [], []
    for layer in range(2):
        wc = wv.at[layer, 1, 0]
        links.arrived(c_y[layer], wc.at[q_me])
        c_r.append(links.start(wc.at[q_me], wc.at[q_me], right))
        c_l.append(links.start(wc.at[q_me], wc.at[q_me], left))
        c_sib[layer].append(links.start(wc.at[q_me], wv.at[layer, 1, 1, q_me], sib))
    for layer in range(2):
        wc = wv.at[layer, 1, 0]
        links.arrived(c_r[layer], wc.at[q_left])
        c_fr.append(links.start(wc.at[halfq(me + 3, 0)], wc.at[halfq(me + 3, 0)], right))
        links.arrived(c_l[layer], wc.at[q_right])
        c_fl.append(links.start(wc.at[halfq(me + 1, 1)], wc.at[halfq(me + 1, 1)], left))
        c_sib[layer].append(links.start(wc.at[q_left], wv.at[layer, 1, 1, q_left], sib))
        c_sib[layer].append(links.start(wc.at[q_right], wv.at[layer, 1, 1, q_right], sib))

    def weights_done(layer):
        wc = wv.at[layer, 1, 0]
        links.arrived(c_fr[layer], wc.at[q_far0])
        links.arrived(c_fl[layer], wc.at[q_far1])
        q_far = quart(me + 2)
        c_sib[layer].append(links.start(wc.at[q_far], wv.at[layer, 1, 1, q_far], sib))
        links.arrived(c_sib[layer][0], wv.at[layer, 0, 1])
        for i, q in zip(c_sib[layer][1:], (q_me, q_left, q_right, q_far)):
            links.arrived(i, wv.at[layer, 1, 1, q])

    def tile(layer, k, cr, j, i):
        return wv[layer, k, cr, pl.ds(pl.multiple_of((2 * j + i) * TILE, TILE), TILE), :]

    def mixed(ref, layer, u):
        return ref[u] * live_s[layer, u] + ref[pair_s[layer, u]] * both_s[layer, u]

    def put(layer, k, cr, j, i, value):
        rows = pl.ds(pl.multiple_of((2 * j + i) * TILE, TILE), TILE)
        if cr == 0:
            gmine[layer, k, rows, :] = value
        else:
            gsend[layer, k, rows, :] = value.astype(bf16)

    groups = [(k, cr) for cr in (1, 0) for k in (0, 1)]

    def project(layer):
        def step(j, carry):
            for k, cr in groups:
                u = slot_of(k, cr, j)
                ct[u] = dot(xv[layer, u], tile(layer, k, cr, j, 0), 1, 0)
            return carry

        lax.fori_loop(0, per_owner, step, 0)

    def middle(layer):
        def step(j, carry):
            for k, cr in groups:
                u = slot_of(k, cr, j)
                value, slope = gelu_pair(mixed(ct, layer, u))
                sl[u] = slope
                active = value.astype(bf16)
                second = tile(layer, k, cr, j, 1)
                delta = dot(active, second, 1, 0)
                cotangent = (loss_scale * (xv[layer, u].astype(f32) + delta)).astype(bf16)
                sp[u] = dot(cotangent, second, 1, 1)
                put(layer, k, cr, j, 1, dot(active, cotangent, 0, 0))
            return carry

        lax.fori_loop(0, per_owner, step, 0)

    def last(layer, cr):
        def step(j, carry):
            for k in (0, 1):
                u = slot_of(k, cr, j)
                grad_pre = (mixed(sp, layer, u) * sl[u]).astype(bf16)
                put(layer, k, cr, j, 0, dot(xv[layer, u], grad_pre, 0, 0))
            return carry

        lax.fori_loop(0, per_owner, step, 0)

    c_g = {}

    def swap(layer):
        for k in range(2):
            c_g[layer, k] = links.start(gsend.at[layer, k], grecv.at[layer, k], sib)

    def join(layer):
        for k in range(2):
            links.arrived(c_g[layer, k], grecv.at[layer, k])

            def step(i, carry, k=k):
                rows = pl.ds(pl.multiple_of(i * chunk_rows, chunk_rows), chunk_rows)
                gsum[layer, k, rows, :] = (gmine[layer, k, rows, :] + grecv[layer, k, rows, :].astype(f32)).astype(bf16)
                return carry

            lax.fori_loop(0, nx, step, 0)

    def part(chunk, wave):
        return pl.ds(pl.multiple_of(lax.rem(chunk, nx) * chunk_rows + wave * sub, sub), sub)

    c_ring = {}
    ways = ((slots_p, right, 1), (slots_m, left, -1))

    def slot_at(d, layer, k, wave, t):
        return ways[d][0].at[layer, k, wave, t]

    def hop(layer, t, waves=range(WAVES)):
        for wave in waves:
            for d in range(2):
                for k in (d, 1 - d):
                    if t == 0 and k != d:
                        continue
                    chunk = part(me + ways[d][2] * (half - t) + nx, wave)
                    if t == 0 or (t == 1 and k != d):
                        src = gsum.at[layer, k, chunk]
                    else:
                        src = slot_at(d, layer, k, wave, t - 1)
                        links.arrived(c_ring[d, layer, k, wave, t - 1], src)
                        src[...] = (src[...].astype(f32) + gsum[layer, k, chunk, :].astype(f32)).astype(bf16)
                    c_ring[d, layer, k, wave, t] = links.start(src, slot_at(d, layer, k, wave, t), ways[d][1])

    c_far = {}

    def finish(layer, wave):
        for k in range(2):
            total = gsum[layer, k, part(me, wave), :].astype(f32)
            for d in range(2):
                src = slot_at(d, layer, k, wave, half - 1)
                links.arrived(c_ring[d, layer, k, wave, half - 1], src)
                total = total + src[...].astype(f32)
            if layer == 0 and k == 0:
                fin[wave] = total
                continue
            i = layer * 2 + k - 1
            ysend[i, wave] = total.astype(bf16)
            device = (y_far, y_same, y_cross)[i]
            c_far[i, wave] = links.start(ysend.at[i, wave], yrecv.at[i, wave], device)

    for load in loads:
        load.wait()
    weights_done(0)
    project(0)
    middle(0)
    last(0, 1)
    swap(0)
    last(0, 0)
    weights_done(1)
    join(0)
    hop(0, 0)
    project(1)
    hop(0, 1)
    middle(1)
    for t in range(2, half):
        hop(0, t)
    last(1, 1)
    swap(1)
    last(1, 0)
    join(1)
    hop(1, 0)
    for wave in range(WAVES):
        finish(0, wave)
    for t in range(1, half):
        hop(1, t)
    for wave in range(WAVES):
        finish(1, wave)

    c_out = {}
    for wave in range(WAVES):
        total = fin[wave]
        for i in range(3):
            links.arrived(c_far[i, wave], yrecv.at[i, wave])
            total = total + yrecv[i, wave].astype(f32)
        mine = part(me, wave)
        outv[mine, :] = total.astype(bf16)
        for d in range(2):
            c_out[d, wave, 1] = links.start(outv.at[mine], outv.at[mine], ways[d][1])
    for t in range(2, half + 1):
        for wave in range(WAVES):
            for d in range(2):
                got = part(me - ways[d][2] * (t - 1) + nx, wave)
                links.arrived(c_out[d, wave, t - 1], outv.at[got])
                if t < half or d == wave % 2:
                    c_out[d, wave, t] = links.start(outv.at[got], outv.at[got], ways[d][1])
    for wave in range(WAVES):
        d = wave % 2
        links.arrived(c_out[d, wave, half], outv.at[part(me + half, wave)])
    store = pltpu.make_async_copy(outv, out, lsem.at[2])
    store.start()
    links.drain()
    store.wait()


def solution(mesh):
    nx, ns = mesh.shape["dp"], mesh.shape["section"]

    def body(x_down, x_up, w_tiles, tile_rows, tile_cols, counts):
        rows, width = x_down.shape[2:]
        layers, per_owner = w_tiles.shape[1:3]
        slots = tile_rows.shape[2]
        big = per_owner * 2 * TILE
        loss_scale = float(2 * rows * nx * mesh.shape["fsdp"]) ** (-0.5)
        f32, bf16 = jnp.float32, jnp.bfloat16
        sub = big // nx // WAVES
        n = copies_of(nx)
        smem = pl.BlockSpec(memory_space=pltpu.SMEM)
        hbm = pl.BlockSpec(memory_space=pl.ANY)
        blocks = pl.pallas_call(
            pick,
            out_shape=jax.ShapeDtypeStruct((2, slots, rows, TILE), bf16),
            in_specs=[smem] + [hbm] * 2,
            out_specs=pl.BlockSpec(memory_space=pltpu.VMEM),
            scratch_shapes=[pltpu.SemaphoreType.DMA((2, slots))],
        )(tile_rows.reshape(2, slots), x_down.reshape(rows, width), x_up.reshape(rows, width))
        pair, live, other_live = slot_pairs(tile_cols.reshape(2, slots), counts.reshape(2, -1))
        total = pl.pallas_call(
            functools.partial(kernel, nx, ns, loss_scale),
            out_shape=jax.ShapeDtypeStruct((big, TILE), bf16),
            in_specs=[smem] * 3 + [hbm] * 2,
            out_specs=hbm,
            scratch_shapes=[
                pltpu.VMEM((2, slots, rows, TILE), bf16),
                pltpu.VMEM((2, 2, 2, big, TILE), bf16),
                pltpu.VMEM((slots, rows, TILE), f32),
                pltpu.VMEM((slots, rows, TILE), f32),
                pltpu.VMEM((slots, rows, TILE), f32),
                pltpu.VMEM((2, 2, big, TILE), f32),
                pltpu.VMEM((2, 2, big, TILE), bf16),
                pltpu.VMEM((2, 2, big, TILE), bf16),
                pltpu.VMEM((2, 2, big, TILE), bf16),
                pltpu.VMEM((2, 2, WAVES, nx // 2, sub, TILE), bf16),
                pltpu.VMEM((2, 2, WAVES, nx // 2, sub, TILE), bf16),
                pltpu.VMEM((3, WAVES, sub, TILE), bf16),
                pltpu.VMEM((3, WAVES, sub, TILE), bf16),
                pltpu.VMEM((WAVES, sub, TILE), f32),
                pltpu.VMEM((big, TILE), bf16),
                pltpu.SemaphoreType.DMA((3,)),
                pltpu.SemaphoreType.DMA((n,)),
                pltpu.SemaphoreType.DMA((n,)),
            ],
            compiler_params=pltpu.CompilerParams(collective_id=0, has_side_effects=True),
        )(
            pair, live.astype(f32), (live * other_live).astype(f32), blocks, w_tiles.reshape(layers, big, TILE),
        )
        return total.reshape(1, per_owner, 2, TILE, TILE)

    in_specs = (
        P("section", "dp", "fsdp", None),
        P("section", "dp", "fsdp", None),
        P("section", None, "fsdp", None, None, None),
        P("section", None, None),
        P("section", None, None),
        P("section", None, None),
    )
    out_specs = P("section", "fsdp", None, None, None)
    return jax.shard_map(body, mesh=mesh, in_specs=in_specs, out_specs=out_specs, check_vma=False)
```

```python
import functools
import math

import jax
import jax.numpy as jnp
from jax import lax
from jax.experimental import pallas as pl
from jax.experimental.pallas import tpu as pltpu
from jax.sharding import PartitionSpec as P

TILE = 128
MESH = pl.DeviceIdType.MESH

tanh_scale = math.sqrt(2.0 / math.pi)
cubic_coef = 0.044715


def gelu_pair(hidden):
    square = hidden * hidden
    inner = hidden * (tanh_scale + (tanh_scale * cubic_coef) * square)
    part = 0.5 + 0.5 * jnp.tanh(inner)
    value = hidden * part
    slope = part + value * (1.0 - part) * (2.0 * tanh_scale + (6.0 * tanh_scale * cubic_coef) * square)
    return value, slope


def dot(a, b, ca, cb):
    return lax.dot_general(a, b, (((ca,), (cb,)), ((), ())), preferred_element_type=jnp.float32)


def pairs(counts_s, cols, pair, live, both):
    f32 = jnp.float32
    slots = cols.shape[1]
    per_owner = slots // counts_s.shape[1]
    down = lax.broadcasted_iota(jnp.int32, (slots, slots), 0)
    along = lax.broadcasted_iota(jnp.int32, (slots, slots), 1)

    def alive(ids, layer):
        held = jnp.zeros_like(ids)
        for o in range(counts_s.shape[1]):
            held = jnp.where(ids >= o * per_owner, counts_s[layer, o] + o * per_owner, held)
        return (ids < held).astype(f32)

    for layer in range(2):
        row = cols[pl.ds(layer, 1), :].astype(f32)
        column = jnp.sum(jnp.where(down == along, row, 0.0), axis=1, keepdims=True)
        same = jnp.where((column == row) & (down != along), 1.0, 0.0)
        mine = alive(along, layer)
        pair[pl.ds(layer, 1), :] = jnp.sum(same * down.astype(f32), axis=0, keepdims=True).astype(jnp.int32)
        live[pl.ds(layer, 1), :] = mine[:1]
        both[pl.ds(layer, 1), :] = jnp.sum(same * alive(down, layer) * mine, axis=0, keepdims=True)


class Links:
    def __init__(self, send_sems, recv_sems):
        self.send_sems, self.recv_sems = send_sems, recv_sems
        self.started = []

    def start(self, src, dst, device):
        i = len(self.started)
        copy = pltpu.make_async_remote_copy(
            src_ref=src, dst_ref=dst, send_sem=self.send_sems.at[i], recv_sem=self.recv_sems.at[i],
            device_id=device, device_id_type=MESH,
        )
        copy.start()
        self.started.append((copy, device))
        return i

    def arrived(self, i, landing):
        device = self.started[i][1]
        pltpu.make_async_remote_copy(
            src_ref=landing, dst_ref=landing, send_sem=self.send_sems.at[i],
            recv_sem=self.recv_sems.at[i], device_id=device, device_id_type=MESH,
        ).wait_recv()

    def drain(self):
        for copy, _ in self.started:
            copy.wait_send()


COPIES = 2 * 10 + 4 + 4 * 8 + 6 + 14


def kernel(nx, ns, loss_scale, rows_s, pair_s, live_s, both_s, x_down, x_up, w, out,
           xv, wv, ct, sp, sl, gmine, gsend, grecv, gsum, near, far, direct, merged, ysend, yrecv, fin, outv,
           xsem, lsem, send_sems, recv_sems):
    f32, bf16 = jnp.float32, jnp.bfloat16
    per_owner = w.shape[1] // (2 * TILE)
    quarter = w.shape[1] // 4
    unit_rows = per_owner * TILE
    sub = unit_rows // nx

    me = lax.axis_index("dp")
    sec = lax.axis_index("section")
    own = lax.axis_index("fsdp")
    hi, core = own // 2, own % 2
    mirror = lax.rem(sec + ns // 2, ns)
    across = lax.rem(own + 2, 4)
    sib = {"fsdp": own + 1 - 2 * core}
    y_same = {"section": mirror}
    y_cross = {"section": mirror, "fsdp": across}
    y_far = {"fsdp": across}

    def along(by):
        return {"dp": lax.rem(me + by + nx, nx)}

    peers = [y_far, sib, y_cross, y_same] + [along(by) for by in range(1, nx)]

    def fetch(b, carry):
        at = pl.ds(pl.multiple_of(b * TILE, TILE), TILE)
        pltpu.make_async_copy(x_down.at[:, at], xv.at[0, b], xsem.at[0, b]).start()
        pltpu.make_async_copy(x_up.at[:, at], xv.at[1, b], xsem.at[1, b]).start()
        return carry

    def fetched(b, carry):
        at = pl.ds(pl.multiple_of(b * TILE, TILE), TILE)
        pltpu.make_async_copy(x_down.at[:, at], xv.at[0, b], xsem.at[0, b]).wait()
        pltpu.make_async_copy(x_up.at[:, at], xv.at[1, b], xsem.at[1, b]).wait()
        return carry

    barrier = pltpu.get_barrier_semaphore()
    for peer in peers:
        pl.semaphore_signal(barrier, inc=1, device_id=peer, device_id_type=MESH)
    load_w = pltpu.make_async_copy(w, wv.at[:, 0, 0], lsem.at[0])
    load_w.start()
    lax.fori_loop(0, xv.shape[1], fetch, 0)
    pl.semaphore_wait(barrier, len(peers))

    links = Links(send_sems, recv_sems)

    def quart(x):
        return pl.ds(pl.multiple_of(lax.rem(x, 4) * quarter, quarter), quarter)

    def halfq(x, second):
        return pl.ds(pl.multiple_of(lax.rem(x, 4) * quarter + second * (quarter // 2), quarter // 2), quarter // 2)

    q_me, q_left, q_right, q_far = quart(me), quart(me + 3), quart(me + 1), quart(me + 2)
    c_w = [{}, {}]
    for layer in range(2):
        c_w[layer]["y"] = links.start(w.at[layer, q_me], wv.at[layer, 1, 0, q_me], y_far)
    for layer in range(2):
        c_w[layer]["own"] = links.start(w.at[layer], wv.at[layer, 0, 1], sib)
    for layer in range(2):
        wc = wv.at[layer, 1, 0]
        links.arrived(c_w[layer]["y"], wc.at[q_me])
        for name, by, at in (("r", 1, q_me), ("l", -1, q_me), ("rr", 2, halfq(me, 0)), ("ll", -2, halfq(me, 1))):
            c_w[layer][name] = links.start(wc.at[at], wc.at[at], along(by))
        c_w[layer]["s_me"] = links.start(wc.at[q_me], wv.at[layer, 1, 1, q_me], sib)

    def pass_on(layer):
        wc = wv.at[layer, 1, 0]
        links.arrived(c_w[layer]["r"], wc.at[q_left])
        c_w[layer]["s_left"] = links.start(wc.at[q_left], wv.at[layer, 1, 1, q_left], sib)
        links.arrived(c_w[layer]["l"], wc.at[q_right])
        c_w[layer]["s_right"] = links.start(wc.at[q_right], wv.at[layer, 1, 1, q_right], sib)
        links.arrived(c_w[layer]["rr"], wc.at[halfq(me + 2, 0)])
        links.arrived(c_w[layer]["ll"], wc.at[halfq(me + 2, 1)])
        c_w[layer]["s_far"] = links.start(wc.at[q_far], wv.at[layer, 1, 1, q_far], sib)

    def weights_done(layer):
        links.arrived(c_w[layer]["own"], wv.at[layer, 0, 1])
        for name, q in (("s_me", q_me), ("s_left", q_left), ("s_right", q_right), ("s_far", q_far)):
            links.arrived(c_w[layer][name], wv.at[layer, 1, 1, q])

    def slot_of(k, cr, j):
        return (lax.rem(hi + k, 2) * 2 + lax.rem(core + cr, 2)) * per_owner + j

    def block(layer, u):
        return xv[layer, rows_s[layer, u]]

    def tile(layer, k, cr, j, i):
        return wv[layer, k, cr, pl.ds(pl.multiple_of((2 * j + i) * TILE, TILE), TILE), :]

    def mixed(ref, layer, u):
        return ref[u] * live_s[layer, u] + ref[pair_s[layer, u]] * both_s[layer, u]

    def put(layer, k, cr, j, i, value):
        rows = pl.ds(pl.multiple_of(j * TILE, TILE), TILE)
        if cr == 0:
            gmine[layer, i, k, rows, :] = value
        else:
            gsend[layer, i, k, rows, :] = value.astype(bf16)

    groups = [(k, cr) for cr in (1, 0) for k in (0, 1)]

    def project(layer):
        def step(j, carry):
            for k, cr in groups:
                u = slot_of(k, cr, j)
                ct[u] = dot(block(layer, u), tile(layer, k, cr, j, 0), 1, 0)
            return carry

        lax.fori_loop(0, per_owner, step, 0)

    def middle(layer):
        def step(j, carry):
            for k, cr in groups:
                u = slot_of(k, cr, j)
                value, slope = gelu_pair(mixed(ct, layer, u))
                sl[u] = slope
                active = value.astype(bf16)
                second = tile(layer, k, cr, j, 1)
                delta = dot(active, second, 1, 0)
                cotangent = (loss_scale * (block(layer, u).astype(f32) + delta)).astype(bf16)
                sp[u] = dot(cotangent, second, 1, 1)
                put(layer, k, cr, j, 1, dot(active, cotangent, 0, 0))
            return carry

        lax.fori_loop(0, per_owner, step, 0)

    def last(layer, cr):
        def step(j, carry):
            for k in (0, 1):
                u = slot_of(k, cr, j)
                grad_pre = (mixed(sp, layer, u) * sl[u]).astype(bf16)
                put(layer, k, cr, j, 0, dot(block(layer, u), grad_pre, 0, 0))
            return carry

        lax.fori_loop(0, per_owner, step, 0)

    c_g, c_t, c_far, c_out = {}, {}, {}, {}

    def swap(u):
        c_g[u] = links.start(gsend.at[u], grecv.at[u], sib)

    def join(u):
        links.arrived(c_g[u], grecv.at[u])

        def step(d, carry):
            rows = pl.ds(pl.multiple_of(d * sub, sub), sub)
            for k in range(2):
                gsum[(*u, d, k)] = (gmine[(*u, k, rows)] + grecv[(*u, k, rows)].astype(f32)).astype(bf16)
            return carry

        lax.fori_loop(0, nx, step, 0)

    def chunk(by):
        return lax.rem(me + by + nx, nx)

    def climb(u):
        for d, s in enumerate((1, -1)):
            c_t[u, d, "far"] = links.start(gsum.at[(*u, chunk(4 * s), d)], far.at[(d, *u)], along(2 * s))
            c_t[u, d, "near"] = links.start(gsum.at[(*u, chunk(3 * s))], near.at[(d, *u)], along(s))
        for d, s in enumerate((1, -1)):
            c_t[u, d, "direct"] = links.start(gsum.at[(*u, chunk(s))], direct.at[(d, *u)], along(s))

    def merge(u):
        for d, s in enumerate((1, -1)):
            links.arrived(c_t[u, d, "near"], near.at[(d, *u)])
            links.arrived(c_t[u, d, "far"], far.at[(d, *u)])
            for k in range(2):
                total = near[(d, *u, k)].astype(f32) + gsum[(*u, chunk(2 * s), k)].astype(f32)
                if k == d:
                    total = total + far[(d, *u)].astype(f32)
                near[(d, *u, k)] = total.astype(bf16)
            c_t[u, d, "merged"] = links.start(near.at[(d, *u)], merged.at[(d, *u)], along(2 * s))

    def finish(u):
        layer, i = u
        for d in range(2):
            links.arrived(c_t[u, d, "direct"], direct.at[(d, *u)])
            links.arrived(c_t[u, d, "merged"], merged.at[(d, *u)])
        for k in range(2):
            total = gsum[(*u, me, k)].astype(f32)
            for d in range(2):
                total = total + direct[(d, *u, k)].astype(f32) + merged[(d, *u, k)].astype(f32)
            if layer == 0 and k == 0:
                fin[i] = total
                continue
            y = layer * 2 + k - 1
            ysend[y, i] = total.astype(bf16)
            c_far[y, i] = links.start(ysend.at[y, i], yrecv.at[y, i], (y_far, y_same, y_cross)[y])

    def part(by):
        return pl.ds(pl.multiple_of(chunk(by) * sub, sub), sub)

    def share(i):
        total = fin[i]
        for y in range(3):
            links.arrived(c_far[y, i], yrecv.at[y, i])
            total = total + yrecv[y, i].astype(f32)
        outv[i, part(0), :] = total.astype(bf16)
        for by in (4, -3, 3, -2, 2, -1, 1):
            c_out[by, i] = links.start(outv.at[i, part(0)], outv.at[i, part(0)], along(by))

    stores = []

    def collect(i):
        for by in (-1, 1, -2, 2, -3, 3, 4):
            links.arrived(c_out[by, i], outv.at[i, part(-by)])
        for j in range(per_owner):
            rows = pl.ds((2 * j + i) * TILE, TILE)
            stores.append(pltpu.make_async_copy(outv.at[i, pl.ds(j * TILE, TILE)], out.at[rows], lsem.at[2 * j + i]))
            stores[-1].start()

    load_w.wait()
    lax.fori_loop(0, xv.shape[1], fetched, 0)
    pass_on(0)
    weights_done(0)
    project(0)
    middle(0)
    swap((0, 1))
    pass_on(1)
    last(0, 1)
    swap((0, 0))
    last(0, 0)
    join((0, 1))
    climb((0, 1))
    weights_done(1)
    project(1)
    join((0, 0))
    climb((0, 0))
    merge((0, 1))
    middle(1)
    swap((1, 1))
    merge((0, 0))
    finish((0, 1))
    last(1, 1)
    swap((1, 0))
    last(1, 0)
    join((1, 1))
    climb((1, 1))
    finish((0, 0))
    join((1, 0))
    climb((1, 0))
    merge((1, 1))
    merge((1, 0))
    finish((1, 1))
    finish((1, 0))
    share(1)
    share(0)
    collect(1)
    collect(0)
    links.drain()
    for store in stores:
        store.wait()


def solution(mesh):
    nx, ns = mesh.shape["dp"], mesh.shape["section"]

    def body(x_down, x_up, w_tiles, tile_rows, tile_cols, counts):
        rows, width = x_down.shape[2:]
        layers, per_owner = w_tiles.shape[1:3]
        slots = tile_rows.shape[2]
        unit = per_owner * TILE
        sub = unit // nx
        loss_scale = float(2 * rows * nx * mesh.shape["fsdp"]) ** (-0.5)
        f32, bf16 = jnp.float32, jnp.bfloat16
        smem = pl.BlockSpec(memory_space=pltpu.SMEM)
        vmem = pl.BlockSpec(memory_space=pltpu.VMEM)
        hbm = pl.BlockSpec(memory_space=pl.ANY)
        table = jax.ShapeDtypeStruct((2, slots), f32)
        pair, live, both = pl.pallas_call(
            pairs,
            out_shape=(jax.ShapeDtypeStruct((2, slots), jnp.int32), table, table),
            in_specs=[smem, vmem],
            out_specs=(vmem, vmem, vmem),
        )(counts.reshape(2, -1), tile_cols.reshape(2, slots))
        total = pl.pallas_call(
            functools.partial(kernel, nx, ns, loss_scale),
            out_shape=jax.ShapeDtypeStruct((2 * unit, TILE), bf16),
            in_specs=[smem] * 4 + [hbm] * 3,
            out_specs=hbm,
            scratch_shapes=[
                pltpu.VMEM((2, width // TILE, rows, TILE), bf16),
                pltpu.VMEM((2, 2, 2, 2 * unit, TILE), bf16),
                pltpu.VMEM((slots, rows, TILE), f32),
                pltpu.VMEM((slots, rows, TILE), f32),
                pltpu.VMEM((slots, rows, TILE), f32),
                pltpu.VMEM((2, 2, 2, unit, TILE), f32),
                pltpu.VMEM((2, 2, 2, unit, TILE), bf16),
                pltpu.VMEM((2, 2, 2, unit, TILE), bf16),
                pltpu.VMEM((2, 2, nx, 2, sub, TILE), bf16),
                pltpu.VMEM((2, 2, 2, 2, sub, TILE), bf16),
                pltpu.VMEM((2, 2, 2, sub, TILE), bf16),
                pltpu.VMEM((2, 2, 2, 2, sub, TILE), bf16),
                pltpu.VMEM((2, 2, 2, 2, sub, TILE), bf16),
                pltpu.VMEM((3, 2, sub, TILE), bf16),
                pltpu.VMEM((3, 2, sub, TILE), bf16),
                pltpu.VMEM((2, sub, TILE), f32),
                pltpu.VMEM((2, unit, TILE), bf16),
                pltpu.SemaphoreType.DMA((2, width // TILE)),
                pltpu.SemaphoreType.DMA((2 * per_owner,)),
                pltpu.SemaphoreType.DMA((COPIES,)),
                pltpu.SemaphoreType.DMA((COPIES,)),
            ],
            compiler_params=pltpu.CompilerParams(collective_id=0, has_side_effects=True),
        )(
            tile_rows.reshape(2, slots), pair, live, both,
            x_down.reshape(rows, width), x_up.reshape(rows, width), w_tiles.reshape(layers, 2 * unit, TILE),
        )
        return total.reshape(1, per_owner, 2, TILE, TILE)

    in_specs = (
        P("section", "dp", "fsdp", None),
        P("section", "dp", "fsdp", None),
        P("section", None, "fsdp", None, None, None),
        P("section", None, None),
        P("section", None, None),
        P("section", None, None),
    )
    out_specs = P("section", "fsdp", None, None, None)
    return jax.shard_map(body, mesh=mesh, in_specs=in_specs, out_specs=out_specs, check_vma=False)
```
